32 devices in a mesh: seq: 16 (over z, y, x), head: 2 (over core).
Axes of the slice: x: 2, y: 2, z: 4, core: 2. Of those that a mesh axis runs over, the one named last changes fastest.
Arguments:
- x_in: bfloat16 [2, 2048, 8192], P(None, 'seq', 'head'), may hold values from -6 to 6
- target: bfloat16 [2, 2048, 8192], P(None, 'seq', 'head'), may hold values from -6 to 6
- b_in: bfloat16 [2, 2048, 1024], P(None, 'seq', 'head'), may hold values from -0.125 to 0.125
- c_in: bfloat16 [2, 2048, 1024], P(None, 'seq', 'head'), may hold values from -0.5 to 0.5
- dt_raw: float32 [2, 128, 2048], P(None, 'head', 'seq'), may hold values from -1 to 2.3
- resets: int32 [2, 2048], P(None, 'seq'), may hold values 0 or 1
- decay_rate: float32 [128], P('head'), may hold values from 0 to 1
- conv_w: float32 [4, 8192], P(None, 'head'), may hold values from -3 to 3
- label: int32 [1], replicated, may hold values from 0 to 1
Outputs:
- loss: float32 [], replicated
- grad_x: bfloat16 [2, 2048, 8192], P(None, 'seq', 'head')
- grad_dt: float32 [2, 128, 2048], P(None, 'head', 'seq')
The draws below stay inside these ranges and needn't reach their ends.
All inputs are finite; a program needn't handle non-finite values. No bound on the sum of `resets` on one device may be relied on, other than what follows from the above.
Results may differ from the reference program's by a relative error of at most 0.001.
Values may be sent and summed in bfloat16 or wider, within the bound.
A program may use at most 320 MiB of HBM per device.

```python
import math
import jax
import jax.numpy as jnp
from jax import lax

HEADS = 128
HEADDIM = 64
DSTATE = 128
GROUPS = 8
KERNEL = 4
SPAN = 128
INNER = 8192
LENGTH = 2048


def draw_decay_rate(key, part):
    pick_key, fast_key, slow_key = jax.random.split(key, 3)
    share = 0.5
    quick = jax.random.bernoulli(pick_key, share, (HEADS,))
    fast = jnp.exp(jax.random.uniform(fast_key, (HEADS,), jnp.float32, math.log(1.0 / 55.0), math.log(1.0 / 33.0)))
    slow = jnp.exp(jax.random.uniform(slow_key, (HEADS,), jnp.float32, math.log(0.2 / LENGTH), math.log(1.2 / LENGTH)))
    return jnp.where(quick, fast, slow).astype(jnp.float32)


def set_ends(values, own_key, least, largest):
    longest = values.shape.index(max(values.shape))
    spots = []
    for shift in (0, 1):
        where = [jax.random.randint(jax.random.fold_in(own_key, axis), (), 0, length) for axis, length in enumerate(values.shape)]
        where[longest] = (where[longest] + shift) % values.shape[longest]
        spots.append(tuple(where))
    return values.at[spots[0]].set(least).at[spots[1]].set(largest)


def level_of(own_key, shape, pieces, low, top_value):
    def one(position, parts):
        heights = jax.random.uniform(jax.random.fold_in(jax.random.fold_in(own_key, 6), position), (parts,), jnp.float32, low / len(pieces), top_value / len(pieces))
        return jnp.repeat(jnp.exp(heights), shape[position] // parts).reshape((-1,) + (1,) * (len(shape) - position - 1))

    factor_of = one(*pieces[0])
    for cut in pieces[1:]:
        factor_of = factor_of * one(*cut)
    return factor_of


def noise(rng, extent, scale, most, shards=(), held_as=jnp.bfloat16):
    drawn = jax.random.normal(rng, extent, jnp.float32) * scale
    if len(shards) > 0:
        drawn = level_of(rng, extent, shards, -0.22, 0.18) * drawn
    return jnp.clip(drawn, min=-most, max=most).astype(held_as)


def setup_inputs(seed: int = 0) -> dict:
    streams_of = jax.random.split(jax.random.key(seed), 10)
    return {
        "x_in": noise(streams_of[0], (2, LENGTH, INNER), 1.0, 6.0, ((1, 16), (2, 2))),
        "target": noise(streams_of[1], (2, LENGTH, INNER), 1.0, 6.0, ((1, 16), (2, 2))),
        "b_in": noise(streams_of[2], (2, LENGTH, GROUPS * DSTATE), LENGTH ** -0.5, 0.125, ((1, 16), (2, 2))),
        "c_in": noise(streams_of[3], (2, LENGTH, GROUPS * DSTATE), DSTATE ** -0.5, 0.5, ((1, 16), (2, 2))),
        "dt_raw": jnp.clip(-1.0 + 3.3 * jax.random.uniform(streams_of[4], (2, HEADS, LENGTH), jnp.float32) ** level_of(streams_of[4], (2, HEADS, LENGTH), ((1, 2), (2, 16)), -0.2, 0.2), -1.0, 2.3),
        "resets": set_ends((jax.random.randint(streams_of[5], (2, LENGTH), 0, LENGTH) < 3).astype(jnp.int32), jax.random.fold_in(streams_of[5], 1), 0, 1),
        "decay_rate": draw_decay_rate(jax.random.fold_in(streams_of[9], 71), 0),
        "conv_w": noise(streams_of[7], (KERNEL, INNER), KERNEL ** -0.5, 3.0, ((1, 2),), jnp.float32),
        "label": jax.random.randint(streams_of[8], (1,), 0, 2).astype(jnp.int32),
    }


HIGH = lax.Precision.HIGHEST

def conv_silu(x_ext, keep_ext, conv_w):
    keep_now = keep_ext[2:][:, None]
    keep_two = keep_now * keep_ext[1:-1][:, None]
    keep_three = keep_two * keep_ext[:-2][:, None]
    pre = conv_w[3] * x_ext[3:] + keep_now * conv_w[2] * x_ext[2:-1]
    pre = pre + keep_two * conv_w[1] * x_ext[1:-2] + keep_three * conv_w[0] * x_ext[:-3]
    return jax.nn.silu(pre)

def ssd_span(state, values, steps, logs, marks, b_rows, c_rows):
    size, heads, width = values.shape
    ratio = heads // b_rows.shape[1]
    running = jnp.cumsum(logs, axis=1)
    seen = jnp.cumsum(marks)
    order = jnp.arange(size)
    valid = (order[:, None] >= order[None, :]) & (seen[:, None] == seen[None, :])
    gap = jnp.where(valid[None], running[:, :, None] - running[:, None, :], 0.0)
    decay = jnp.where(valid[None], jnp.exp(gap), 0.0)
    scores = jnp.einsum('ign,jgn->gij', c_rows, b_rows, precision=HIGH)
    scores = jnp.repeat(scores, ratio, axis=0)
    mixing = decay * scores * steps[:, None, :]
    intra = jnp.einsum('hij,jhp->ihp', mixing, values, precision=HIGH)
    b_heads = jnp.repeat(b_rows, ratio, axis=1)
    c_heads = jnp.repeat(c_rows, ratio, axis=1)
    entry = jnp.exp(running) * (seen == 0.0).astype(running.dtype)[None, :]
    carried = jnp.einsum('ihn,hpn->ihp', c_heads, state, precision=HIGH) * entry.T[:, :, None]
    tail = jnp.exp(running[:, -1:] - running) * (seen[-1] == seen).astype(running.dtype)[None, :] * steps
    weighted = values * tail.T[:, :, None]
    final = entry[:, -1][:, None, None] * state + jnp.einsum('jhp,jhn->hpn', weighted, b_heads, precision=HIGH)
    return (final, intra + carried)

def mixer_rows(state, values, steps, logs, marks, b_rows, c_rows, saving):
    rows, heads, width = values.shape
    count = rows // SPAN

    def blocks(array):
        return array.reshape((count, SPAN) + array.shape[1:])

    def blocks_heads(array):
        return array.reshape(heads, count, SPAN).transpose(1, 0, 2)
    step_fn = jax.checkpoint(ssd_span) if saving else ssd_span

    def advance(carry, block):
        return step_fn(carry, *block)
    final, outs = lax.scan(advance, state, (blocks(values), blocks_heads(steps), blocks_heads(logs), blocks(marks), blocks(b_rows), blocks(c_rows)))
    return (outs.reshape(rows, heads * width), final)

def local_pass(x_ext, raw, state, keep_ext, marks, b_rows, c_rows, conv_w, decay_rate, saving):
    rows = x_ext.shape[0] - 3
    heads = raw.shape[0]
    values = conv_silu(x_ext, keep_ext, conv_w).reshape(rows, heads, -1)
    steps = jax.nn.softplus(raw)
    logs = -steps * decay_rate[:, None]
    return mixer_rows(state, values, steps, logs, marks, b_rows, c_rows, saving)

def reference(x_in, target, b_in, c_in, dt_raw, resets, decay_rate, conv_w, label):
    marks = resets.astype(jnp.float32)
    keep_ext = jnp.concatenate([jnp.ones((2, 2), jnp.float32), 1.0 - marks], axis=1)
    b_rows = b_in.astype(jnp.float32).reshape(2, LENGTH, GROUPS, DSTATE)
    c_rows = c_in.astype(jnp.float32).reshape(2, LENGTH, GROUPS, DSTATE)
    target_f = target.astype(jnp.float32)
    count = LENGTH * INNER
    sign = jnp.where(jnp.arange(2) == label[0], 1.0, -1.0).astype(jnp.float32)

    def single(x_one, raw_one, state_one, keep_one, marks_one, b_one, c_one):
        return local_pass(x_one, raw_one, state_one, keep_one, marks_one, b_one, c_one, conv_w, decay_rate, True)

    def objective(x_full, raw_full):
        x_ext = jnp.concatenate([jnp.zeros((2, 3, INNER), jnp.float32), x_full], axis=1)
        start = jnp.zeros((2, HEADS, HEADDIM, DSTATE), jnp.float32)
        outs, finals = jax.vmap(single)(x_ext, raw_full, start, keep_ext, marks, b_rows, c_rows)
        scores = lax.optimization_barrier(jnp.sum(outs * target_f, axis=(1, 2))) / math.sqrt(count)
        margin = jnp.sum(sign * scores)
        return jax.nn.softplus(-margin)
    loss, pullback = jax.vjp(objective, x_in.astype(jnp.float32), dt_raw)
    grad_x, grad_dt = pullback(jnp.ones_like(loss) * math.sqrt(count))
    return (loss, grad_x.astype(jnp.bfloat16), grad_dt)
```

```python
import functools
import math

import jax
import jax.numpy as jnp
from jax import lax
from jax.experimental import pallas as pl
from jax.experimental.pallas import tpu as pltpu
from jax.sharding import Mesh
from jax.sharding import PartitionSpec as P

DSTATE = 128
SPAN = 128
LANES = 128
TAPS = 4
HALO = 16
FAR = -1e30
HIGH = lax.Precision.HIGHEST
F32 = jnp.float32
BF16 = jnp.bfloat16


def split(value):
    high = value.astype(BF16)
    low = (value - high.astype(F32)).astype(BF16)
    return high, low


def mm(left, right):
    return lax.dot_general(left, right, (((1,), (0,)), ((), ())), preferred_element_type=F32)


def mm_exact_left(left, right):
    high, low = split(right)
    return mm(left, high) + mm(left, low)


def mm_exact_right(left, right):
    high, low = split(left)
    return mm(high, right) + mm(low, right)


def spread_matrix(offset, chans, width):
    row = lax.broadcasted_iota(jnp.int32, (LANES, chans), 0)
    head = lax.broadcasted_iota(jnp.int32, (LANES, chans), 1) // width
    return jnp.where(row == head + offset, 1.0, 0.0).astype(BF16)


def gather_matrix(chans, width):
    head = lax.broadcasted_iota(jnp.int32, (chans, LANES), 0) // width
    col = lax.broadcasted_iota(jnp.int32, (chans, LANES), 1)
    return jnp.where(col == head, 1.0, 0.0).astype(BF16)


def conv_of(x_ref, xe_scr, w_ref, tok, lane, first):
    xe_scr[...] = x_ref[pl.ds(first, SPAN + HALO), :].astype(F32)
    pre = w_ref[3:4, :] * xe_scr[pl.ds(HALO, SPAN), :]
    for back in range(1, TAPS):
        scale = tok[:, lane + back - 1 : lane + back] * w_ref[3 - back : 4 - back, :]
        pre = pre + scale * xe_scr[pl.ds(HALO - back, SPAN), :]
    return pre


def ends_kernel(heads, count, x_ref, t_ref, bt_ref, ct_ref, tok_ref, w_ref, alone_ref, seed_ref, xe_scr):
    chans = x_ref.shape[1]
    width = chans // heads
    spread_entry = spread_matrix(heads, chans, width)
    spread_tail = spread_matrix(3 * heads, chans, width)
    alone_ref[...] = jnp.zeros_like(alone_ref)
    seed_ref[...] = jnp.zeros_like(seed_ref)

    def forward(k, carry):
        first = pl.multiple_of(k * SPAN, SPAN)
        tok = tok_ref[pl.ds(first, SPAN), :]
        values = jax.nn.silu(conv_of(x_ref, xe_scr, w_ref, tok, 5 * heads, first))
        weighted = values * mm_exact_right(tok, spread_tail)
        through = mm_exact_right(tok[SPAN - 8 :, :], spread_entry)[7:8, :]
        added = mm_exact_left(bt_ref[:, pl.ds(first, SPAN)], weighted)
        alone_ref[...] = through * alone_ref[...] + added
        return carry

    lax.fori_loop(0, count, forward, 0)

    def backward(step, carry):
        first = pl.multiple_of((count - 1 - step) * SPAN, SPAN)
        tok = tok_ref[pl.ds(first, SPAN), :]
        entry = mm_exact_right(tok, spread_entry)
        weighted = entry * t_ref[pl.ds(first, SPAN), :].astype(F32)
        added = mm_exact_left(ct_ref[:, pl.ds(first, SPAN)], weighted)
        seed_ref[...] = entry[SPAN - 1 : SPAN, :] * seed_ref[...] + added
        return carry

    lax.fori_loop(0, count, backward, 0)


def main_kernel(
    heads, count, x_ref, t_ref, b_ref, c_ref, bt_ref, ct_ref, tok_ref, row_ref, w_ref, rate_ref,
    start_ref, later_ref, grad_ref, ddt_ref, score_ref, xe_scr, s_scr, g_scr, v_scr, y_scr, d_scr, cv_scr,
):
    chans = x_ref.shape[1]
    width = chans // heads
    per = LANES // width
    spread_steps = spread_matrix(0, chans, width)
    spread_entry = spread_matrix(heads, chans, width)
    spread_reach = spread_matrix(2 * heads, chans, width)
    spread_tail = spread_matrix(3 * heads, chans, width)
    gather = gather_matrix(chans, width)
    s_scr[0] = start_ref[...]
    g_scr[...] = later_ref[...]
    score_ref[...] = jnp.zeros_like(score_ref)
    cv_scr[...] = jnp.zeros_like(cv_scr)
    total = count * SPAN
    grad_ref[pl.ds(total, HALO), :] = jnp.zeros((HALO, chans), F32)

    def forward(k, carry):
        first = pl.multiple_of(k * SPAN, SPAN)
        tok = tok_ref[pl.ds(first, SPAN), :]
        pre = conv_of(x_ref, xe_scr, w_ref, tok, 5 * heads, first)
        v_scr[pl.ds(first, SPAN), :] = pre
        weighted = jax.nn.silu(pre) * mm_exact_right(tok, spread_tail)
        through = mm_exact_right(tok[SPAN - 8 :, :], spread_entry)[7:8, :]
        added = mm_exact_left(bt_ref[:, pl.ds(first, SPAN)], weighted)
        s_scr[k + 1] = through * s_scr[k] + added
        return carry

    lax.fori_loop(0, count, forward, 0)

    def backward(step, carry):
        k = count - 1 - step
        first = pl.multiple_of(k * SPAN, SPAN)
        here = pl.ds(first, SPAN)
        tok = tok_ref[here, :]
        pre = v_scr[here, :]
        sig = jax.nn.sigmoid(pre)
        values = pre * sig
        slope = sig * (1.0 + pre * (1.0 - sig))
        target = t_ref[here, :]
        b_rows = b_ref[here, :]
        c_rows = c_ref[here, :]
        bt = bt_ref[:, here]
        ct = ct_ref[:, here]
        steps = mm_exact_right(tok, spread_steps)
        entry = mm_exact_right(tok, spread_entry)
        reach = mm_exact_right(tok, spread_reach)
        y_scr[...] = entry * mm_exact_left(c_rows, s_scr[k])
        d_scr[...] = reach * mm_exact_left(b_rows, g_scr[...])
        u_high, u_low = split(steps * values)
        scores = mm(c_rows, bt)
        scores_t = mm(b_rows, ct)
        seen_col = tok[:, 5 * heads + 3 : 5 * heads + 4]
        seen_row = row_ref[5 * heads + 3 : 5 * heads + 4, here]
        order_row = lax.broadcasted_iota(jnp.int32, (SPAN, SPAN), 0)
        order_col = lax.broadcasted_iota(jnp.int32, (SPAN, SPAN), 1)
        same = seen_col == seen_row
        valid = same & (order_row >= order_col)
        valid_t = same & (order_row <= order_col)
        lane = lax.broadcasted_iota(jnp.int32, (SPAN, LANES), 1) // width
        for unit in range(heads // per):
            cols = slice(unit * LANES, (unit + 1) * LANES)
            t_unit = target[:, cols]
            both = jnp.concatenate([u_high[:, cols], u_low[:, cols]], axis=1)
            y_unit = jnp.zeros((SPAN, LANES), F32)
            d_unit = jnp.zeros((SPAN, LANES), F32)
            for part in range(per):
                h = 4 * heads + unit * per + part
                r_col = tok[:, h : h + 1]
                r_row = row_ref[h : h + 1, here]
                gap = r_col - r_row
                mix = jnp.exp(jnp.where(valid, gap, FAR)) * scores
                mix_t = jnp.exp(jnp.where(valid_t, -gap, FAR)) * scores_t
                m_high, m_low = split(mix)
                n_high, n_low = split(mix_t)
                wide = mm(m_high, both)
                y_part = wide[:, :LANES] + wide[:, LANES:] + mm(m_low, both[:, :LANES])
                d_part = mm(n_high, t_unit) + mm(n_low, t_unit)
                y_unit = jnp.where(lane == part, y_part, y_unit)
                d_unit = jnp.where(lane == part, d_part, d_unit)
            y_scr[:, cols] += y_unit
            d_scr[:, cols] += d_unit
        target_f = target.astype(F32)
        read = y_scr[...] * target_f
        score_ref[...] += jnp.sum(read.reshape(SPAN // 8, 8, chans), axis=0)
        du = d_scr[...]
        by_read = mm_exact_right(read, gather)
        by_step = mm_exact_right(values * du, gather)
        cross = jnp.sum((s_scr[k + 1] * g_scr[...]).reshape(DSTATE // 8, 8, chans), axis=0)
        crossed = jnp.sum(mm_exact_right(cross, gather), axis=0, keepdims=True)
        upper = jnp.where(order_row <= order_col, 1.0, 0.0).astype(BF16)
        d_log = mm_exact_left(upper, by_read - tok * by_step) + crossed
        ddt_ref[here, :] = by_step - rate_ref[...] * d_log
        d_pre = steps * du * slope
        cv_scr[0, pl.ds(HALO, SPAN), :] = w_ref[3:4, :] * d_pre
        for back in range(1, TAPS):
            scale = tok[:, 5 * heads + back - 1 : 5 * heads + back] * w_ref[3 - back : 4 - back, :]
            cv_scr[back, pl.ds(HALO, SPAN), :] = scale * d_pre
        top = cv_scr[0, pl.ds(0, SPAN), :]
        end = cv_scr[0, pl.ds(SPAN, HALO), :]
        for back in range(1, TAPS):
            top = top + cv_scr[back, pl.ds(back, SPAN), :]
            end = end + cv_scr[back, pl.ds(SPAN + back, HALO), :]
        grad_ref[here, :] = top
        tail = pl.ds(pl.multiple_of(first + SPAN, SPAN), HALO)
        grad_ref[tail, :] += end
        weighted = entry * target_f
        g_scr[...] = entry[SPAN - 1 : SPAN, :] * g_scr[...] + mm_exact_left(ct, weighted)
        return carry

    lax.fori_loop(0, count, backward, 0)


def per_pair(shape):
    return pl.BlockSpec((None,) + tuple(shape), lambda b: (b,) + (0,) * len(shape))


def whole(shape):
    return pl.BlockSpec(tuple(shape), lambda b: (0,) * len(shape))


def ends(x_ext, target, b_t, c_t, tok, taps, heads):
    pairs, rows, chans = target.shape
    out = jax.ShapeDtypeStruct((pairs, DSTATE, chans), F32)
    return pl.pallas_call(
        functools.partial(ends_kernel, heads, rows // SPAN),
        grid=(pairs,),
        out_shape=(out, out),
        in_specs=[per_pair(a.shape[1:]) for a in (x_ext, target, b_t, c_t, tok)] + [whole(taps.shape)],
        out_specs=(per_pair(out.shape[1:]),) * 2,
        scratch_shapes=[pltpu.VMEM((SPAN + HALO, chans), F32)],
        name="ends",
    )(x_ext, target, b_t, c_t, tok, taps)


def main(x_ext, target, b_rows, c_rows, b_t, c_t, tok, table, taps, rate, start, later, heads):
    pairs, rows, chans = target.shape
    count = rows // SPAN
    outs = (
        jax.ShapeDtypeStruct((pairs, rows + HALO, chans), F32),
        jax.ShapeDtypeStruct((pairs, rows, LANES), F32),
        jax.ShapeDtypeStruct((pairs, 8, chans), F32),
    )
    return pl.pallas_call(
        functools.partial(main_kernel, heads, count),
        grid=(pairs,),
        out_shape=outs,
        in_specs=[per_pair(a.shape[1:]) for a in (x_ext, target, b_rows, c_rows, b_t, c_t, tok, table)]
        + [whole(taps.shape), whole(rate.shape)]
        + [per_pair(start.shape[1:])] * 2,
        out_specs=tuple(per_pair(o.shape[1:]) for o in outs),
        scratch_shapes=[
            pltpu.VMEM((SPAN + HALO, chans), F32),
            pltpu.VMEM((count + 1, DSTATE, chans), F32),
            pltpu.VMEM((DSTATE, chans), F32),
            pltpu.VMEM((rows, chans), F32),
            pltpu.VMEM((SPAN, chans), F32),
            pltpu.VMEM((SPAN, chans), F32),
            pltpu.VMEM((TAPS, SPAN + 2 * HALO, chans), F32),
        ],
        name="main",
    )(x_ext, target, b_rows, c_rows, b_t, c_t, tok, table, taps, rate, start, later)


def chain(through, alone, axis, backward):
    count = lax.axis_size(axis)
    mine = lax.axis_index(axis)
    if backward:
        mine = count - 1 - mine
    carried = jnp.zeros_like(alone)

    def hop(step, carried):
        leaving = through * carried + alone
        if backward:
            route = [(i, i - 1) for i in range(1, count)]
        else:
            route = [(i, i + 1) for i in range(count - 1)]
        arrived = lax.ppermute(leaving, axis, route)
        return jnp.where(mine == step, arrived, carried)

    if count <= 8:
        for step in range(1, count):
            leaving = through * carried + alone
            source, goal = (count - step, count - step - 1) if backward else (step - 1, step)
            arrived = lax.ppermute(leaving, axis, [(source, goal)])
            carried = jnp.where(mine == step, arrived, carried)
        return carried
    return lax.fori_loop(1, count, hop, carried)


def body(outer, inner, x_in, target, b_in, c_in, dt_raw, resets, decay_rate, conv_w, label):
    rows = x_in.shape[1]
    all_heads = dt_raw.shape[1]
    width = x_in.shape[2] // all_heads
    parts = lax.axis_size(inner)
    heads = all_heads // parts
    chans = heads * width
    states = b_in.shape[2] // parts
    tokens = rows * parts
    count = tokens // SPAN
    mine = lax.axis_index(inner)

    def exchange(array):
        if parts == 1:
            return array
        return lax.all_to_all(array, inner, 0, 0, tiled=True)

    def cut(array):
        return array.reshape(2, rows, parts, -1)

    packed = jnp.concatenate([cut(x_in), cut(target), cut(b_in), cut(c_in)], axis=3)
    packed = exchange(packed.transpose(2, 0, 1, 3))
    packed = packed.transpose(1, 0, 2, 3).reshape(2, tokens, -1)
    x_all = packed[:, :, :chans]
    t_all = packed[:, :, chans : 2 * chans]
    b_all = packed[:, :, 2 * chans : 2 * chans + states]
    c_all = packed[:, :, 2 * chans + states :]
    marks = resets.astype(F32)
    small = jnp.concatenate(
        [dt_raw.reshape(2, parts, heads, rows), jnp.broadcast_to(marks[:, None, None, :], (2, parts, 1, rows))], axis=2
    )
    small = exchange(small.transpose(1, 0, 2, 3))
    small = small.transpose(1, 2, 0, 3).reshape(2, heads + 1, tokens)
    raw = small[:, :heads]
    marks = small[:, heads]
    planes = lax.axis_size(outer)
    ahead = [(i, i + 1) for i in range(planes - 1)]
    edge_rows = lax.ppermute(x_all[:, tokens - HALO :], outer, ahead)
    edge_marks = lax.ppermute(marks[:, tokens - 2 :], outer, ahead)
    x_ext = jnp.concatenate([edge_rows, x_all], axis=1)
    keep = 1.0 - jnp.concatenate([edge_marks, marks], axis=1)
    keep_one = keep[:, 2:]
    keep_two = keep_one * keep[:, 1:-1]
    keep_three = keep_two * keep[:, :-2]
    rate = lax.dynamic_slice(decay_rate, (mine * heads,), (heads,))
    taps = lax.dynamic_slice(conv_w, (0, mine * chans), (TAPS, chans))
    steps = jax.nn.softplus(raw)
    logs = -steps * rate[None, :, None]
    upto = jnp.tril(jnp.ones((SPAN, SPAN), F32))
    both = jnp.concatenate([logs, marks[:, None]], axis=1).reshape(2, heads + 1, count, SPAN)
    sums = jnp.einsum("bhkj,ij->bhki", both, upto, precision=HIGH)
    running = sums[:, :heads]
    seen = jnp.round(sums[:, heads:])
    entry = jnp.exp(running) * (seen == 0.0).astype(F32)
    reach = jnp.exp(running[..., -1:] - running) * (seen[..., -1:] == seen).astype(F32)
    through = jnp.prod(entry[..., -1], axis=2)

    def flat(array):
        return array.reshape(2, -1, tokens)

    used = 5 * heads + 4
    table = jnp.concatenate(
        [
            steps,
            flat(entry),
            flat(reach),
            flat(reach) * steps,
            flat(running),
            keep_one[:, None],
            keep_two[:, None],
            keep_three[:, None],
            flat(seen),
            jnp.zeros((2, LANES - used, tokens), F32),
        ],
        axis=1,
    )
    tok = table.transpose(0, 2, 1)
    b_t = b_all.transpose(0, 2, 1)
    c_t = c_all.transpose(0, 2, 1)
    alone, seed = ends(x_ext, t_all, b_t, c_t, tok, taps, heads)
    wide = jnp.repeat(through, width, axis=1)[:, None, :]
    start = chain(wide, alone, outer, False)
    later = chain(wide, seed, outer, True)
    rate_row = jnp.pad(rate, (0, LANES - heads))[None]
    grad, ddt, score = main(x_ext, t_all, b_all, c_all, b_t, c_t, tok, table, taps, rate_row, start, later, heads)
    totals = lax.psum(jnp.sum(score, axis=(1, 2)), (outer, inner, "head"))
    size = tokens * planes * x_in.shape[2] * lax.axis_size("head")
    scores = totals / math.sqrt(size)
    sign = jnp.where(jnp.arange(2) == label[0], 1.0, -1.0).astype(F32)
    margin = jnp.sum(sign * scores)
    loss = jax.nn.softplus(-margin)
    factor = -jax.nn.sigmoid(-margin) * sign
    back_rows = lax.ppermute(grad[:, :HALO], outer, [(i + 1, i) for i in range(planes - 1)])
    grad = grad[:, HALO:]
    grad = jnp.concatenate([grad[:, : tokens - HALO], grad[:, tokens - HALO :] + back_rows], axis=1)
    grad = (factor[:, None, None] * grad).astype(BF16)
    grad = exchange(grad.reshape(2, parts, rows, chans).transpose(1, 0, 2, 3))
    grad = grad.transpose(1, 2, 0, 3).reshape(2, rows, parts * chans)
    grad_raw = factor[:, None, None] * jax.nn.sigmoid(raw) * ddt[:, :, :heads].transpose(0, 2, 1)
    grad_raw = exchange(grad_raw.reshape(2, heads, parts, rows).transpose(2, 0, 1, 3))
    grad_raw = grad_raw.transpose(1, 0, 2, 3).reshape(2, all_heads, rows)
    return (loss, grad, grad_raw)


def solution(mesh):
    def program(*arrays):
        ways, across = mesh.shape["seq"], mesh.shape["head"]
        groups = arrays[2].shape[2] // DSTATE // across
        parts = math.gcd(groups, ways)
        devices = mesh.devices.reshape(ways // parts, parts, across)
        finer = Mesh(devices, ("outer", "inner", "head"))
        seq = ("outer", "inner")
        in_specs = (
            P(None, seq, "head"),
            P(None, seq, "head"),
            P(None, seq, "head"),
            P(None, seq, "head"),
            P(None, "head", seq),
            P(None, seq),
            P("head"),
            P(None, "head"),
            P(),
        )
        out_specs = (P(), P(None, seq, "head"), P(None, "head", seq))
        inner = functools.partial(body, "outer", "inner")
        mapped = jax.shard_map(inner, mesh=finer, in_specs=in_specs, out_specs=out_specs, check_vma=False)
        return mapped(*arrays)

    return program
```

```python
import functools
import math

import jax
import jax.numpy as jnp
from jax import lax
from jax.experimental import pallas as pl
from jax.experimental.pallas import tpu as pltpu
from jax.sharding import Mesh
from jax.sharding import PartitionSpec as P

DSTATE = 128
SPAN = 128
LANES = 128
TAPS = 4
CUTS = 4
HALO = 16
FAR = -1e30
HIGH = lax.Precision.HIGHEST
F32 = jnp.float32
BF16 = jnp.bfloat16


def split(value):
    high = value.astype(BF16)
    low = (value - high.astype(F32)).astype(BF16)
    return high, low


def mm(left, right):
    return lax.dot_general(left, right, (((1,), (0,)), ((), ())), preferred_element_type=F32)


def mm_exact_left(left, right):
    high, low = split(right)
    return mm(left, high) + mm(left, low)


def mm_exact_right(left, right):
    high, low = split(left)
    return mm(high, right) + mm(low, right)


def spread_matrix(offset, chans, width):
    row = lax.broadcasted_iota(jnp.int32, (LANES, chans), 0)
    head = lax.broadcasted_iota(jnp.int32, (LANES, chans), 1) // width
    return jnp.where(row == head + offset, 1.0, 0.0).astype(BF16)


def gather_matrix(chans, width):
    head = lax.broadcasted_iota(jnp.int32, (chans, LANES), 0) // width
    col = lax.broadcasted_iota(jnp.int32, (chans, LANES), 1)
    return jnp.where(col == head, 1.0, 0.0).astype(BF16)


def conv_of(x_ref, xe_scr, w_ref, tok, lane, first):
    xe_scr[...] = x_ref[pl.ds(first, SPAN + HALO), :].astype(F32)
    pre = w_ref[3:4, :] * xe_scr[pl.ds(HALO, SPAN), :]
    for back in range(1, TAPS):
        scale = tok[:, lane + back - 1 : lane + back] * w_ref[3 - back : 4 - back, :]
        pre = pre + scale * xe_scr[pl.ds(HALO - back, SPAN), :]
    return pre


def ends_kernel(heads, count, x_ref, t_ref, bt_ref, ct_ref, tok_ref, w_ref, alone_ref, seed_ref, xe_scr):
    chans = x_ref.shape[1]
    width = chans // heads
    spread_entry = spread_matrix(heads, chans, width)
    spread_tail = spread_matrix(3 * heads, chans, width)
    alone_ref[...] = jnp.zeros_like(alone_ref)
    seed_ref[...] = jnp.zeros_like(seed_ref)

    def forward(k, carry):
        first = pl.multiple_of(k * SPAN, SPAN)
        tok = tok_ref[pl.ds(first, SPAN), :]
        values = jax.nn.silu(conv_of(x_ref, xe_scr, w_ref, tok, 5 * heads, first))
        weighted = values * mm_exact_right(tok, spread_tail)
        through = mm_exact_right(tok[SPAN - 8 :, :], spread_entry)[7:8, :]
        added = mm_exact_left(bt_ref[:, pl.ds(first, SPAN)], weighted)
        alone_ref[...] = through * alone_ref[...] + added
        return carry

    lax.fori_loop(0, count, forward, 0)

    def backward(step, carry):
        first = pl.multiple_of((count - 1 - step) * SPAN, SPAN)
        tok = tok_ref[pl.ds(first, SPAN), :]
        entry = mm_exact_right(tok, spread_entry)
        weighted = entry * t_ref[pl.ds(first, SPAN), :].astype(F32)
        added = mm_exact_left(ct_ref[:, pl.ds(first, SPAN)], weighted)
        seed_ref[...] = entry[SPAN - 1 : SPAN, :] * seed_ref[...] + added
        return carry

    lax.fori_loop(0, count, backward, 0)


def main_kernel(
    heads, count, x_ref, t_ref, b_ref, c_ref, bt_ref, ct_ref, tok_ref, row_ref, w_ref, rate_ref,
    start_ref, later_ref, grad_ref, ddt_ref, score_ref, xe_scr, s_scr, g_scr, v_scr, y_scr, d_scr, cv_scr,
):
    chans = x_ref.shape[1]
    width = chans // heads
    per = LANES // width
    spread_steps = spread_matrix(0, chans, width)
    spread_entry = spread_matrix(heads, chans, width)
    spread_reach = spread_matrix(2 * heads, chans, width)
    spread_tail = spread_matrix(3 * heads, chans, width)
    gather = gather_matrix(chans, width)
    s_scr[0] = start_ref[...]
    g_scr[...] = later_ref[...]
    score_ref[...] = jnp.zeros_like(score_ref)
    cv_scr[...] = jnp.zeros_like(cv_scr)
    total = count * SPAN
    grad_ref[pl.ds(total, HALO), :] = jnp.zeros((HALO, chans), F32)

    def forward(k, carry):
        first = pl.multiple_of(k * SPAN, SPAN)
        tok = tok_ref[pl.ds(first, SPAN), :]
        pre = conv_of(x_ref, xe_scr, w_ref, tok, 5 * heads, first)
        v_scr[pl.ds(first, SPAN), :] = pre
        weighted = jax.nn.silu(pre) * mm_exact_right(tok, spread_tail)
        through = mm_exact_right(tok[SPAN - 8 :, :], spread_entry)[7:8, :]
        added = mm_exact_left(bt_ref[:, pl.ds(first, SPAN)], weighted)
        s_scr[k + 1] = through * s_scr[k] + added
        return carry

    lax.fori_loop(0, count, forward, 0)

    def backward(step, carry):
        k = count - 1 - step
        first = pl.multiple_of(k * SPAN, SPAN)
        here = pl.ds(first, SPAN)
        tok = tok_ref[here, :]
        pre = v_scr[here, :]
        sig = jax.nn.sigmoid(pre)
        values = pre * sig
        slope = sig * (1.0 + pre * (1.0 - sig))
        target = t_ref[here, :]
        b_rows = b_ref[here, :]
        c_rows = c_ref[here, :]
        bt = bt_ref[:, here]
        ct = ct_ref[:, here]
        steps = mm_exact_right(tok, spread_steps)
        entry = mm_exact_right(tok, spread_entry)
        reach = mm_exact_right(tok, spread_reach)
        y_scr[...] = entry * mm_exact_left(c_rows, s_scr[k])
        d_scr[...] = reach * mm_exact_left(b_rows, g_scr[...])
        u_high, u_low = split(steps * values)
        scores = mm(c_rows, bt)
        scores_t = mm(b_rows, ct)
        seen_col = tok[:, 5 * heads + 3 : 5 * heads + 4]
        seen_row = row_ref[5 * heads + 3 : 5 * heads + 4, here]
        order_row = lax.broadcasted_iota(jnp.int32, (SPAN, SPAN), 0)
        order_col = lax.broadcasted_iota(jnp.int32, (SPAN, SPAN), 1)
        same = seen_col == seen_row
        valid = same & (order_row >= order_col)
        valid_t = same & (order_row <= order_col)
        lane = lax.broadcasted_iota(jnp.int32, (SPAN, LANES), 1) // width
        for unit in range(heads // per):
            cols = slice(unit * LANES, (unit + 1) * LANES)
            t_unit = target[:, cols]
            both = jnp.concatenate([u_high[:, cols], u_low[:, cols]], axis=1)
            y_unit = jnp.zeros((SPAN, LANES), F32)
            d_unit = jnp.zeros((SPAN, LANES), F32)
            for part in range(per):
                h = 4 * heads + unit * per + part
                r_col = tok[:, h : h + 1]
                r_row = row_ref[h : h + 1, here]
                gap = r_col - r_row
                mix = jnp.exp(jnp.where(valid, gap, FAR)) * scores
                mix_t = jnp.exp(jnp.where(valid_t, -gap, FAR)) * scores_t
                m_high, m_low = split(mix)
                n_high, n_low = split(mix_t)
                wide = mm(m_high, both)
                y_part = wide[:, :LANES] + wide[:, LANES:] + mm(m_low, both[:, :LANES])
                d_part = mm(n_high, t_unit) + mm(n_low, t_unit)
                y_unit = jnp.where(lane == part, y_part, y_unit)
                d_unit = jnp.where(lane == part, d_part, d_unit)
            y_scr[:, cols] += y_unit
            d_scr[:, cols] += d_unit
        target_f = target.astype(F32)
        read = y_scr[...] * target_f
        score_ref[...] += jnp.sum(read.reshape(SPAN // 8, 8, chans), axis=0)
        du = d_scr[...]
        by_read = mm_exact_right(read, gather)
        by_step = mm_exact_right(values * du, gather)
        cross = jnp.sum((s_scr[k + 1] * g_scr[...]).reshape(DSTATE // 8, 8, chans), axis=0)
        crossed = jnp.sum(mm_exact_right(cross, gather), axis=0, keepdims=True)
        upper = jnp.where(order_row <= order_col, 1.0, 0.0).astype(BF16)
        d_log = mm_exact_left(upper, by_read - tok * by_step) + crossed
        ddt_ref[here, :] = by_step - rate_ref[...] * d_log
        d_pre = steps * du * slope
        cv_scr[0, pl.ds(HALO, SPAN), :] = w_ref[3:4, :] * d_pre
        for back in range(1, TAPS):
            scale = tok[:, 5 * heads + back - 1 : 5 * heads + back] * w_ref[3 - back : 4 - back, :]
            cv_scr[back, pl.ds(HALO, SPAN), :] = scale * d_pre
        top = cv_scr[0, pl.ds(0, SPAN), :]
        end = cv_scr[0, pl.ds(SPAN, HALO), :]
        for back in range(1, TAPS):
            top = top + cv_scr[back, pl.ds(back, SPAN), :]
            end = end + cv_scr[back, pl.ds(SPAN + back, HALO), :]
        grad_ref[here, :] = top
        tail = pl.ds(pl.multiple_of(first + SPAN, SPAN), HALO)
        grad_ref[tail, :] += end
        weighted = entry * target_f
        g_scr[...] = entry[SPAN - 1 : SPAN, :] * g_scr[...] + mm_exact_left(ct, weighted)
        return carry

    lax.fori_loop(0, count, backward, 0)


def per_pair(shape):
    return pl.BlockSpec((None,) + tuple(shape), lambda b: (b,) + (0,) * len(shape))


def whole(shape):
    return pl.BlockSpec(tuple(shape), lambda b: (0,) * len(shape))


def ends(x_ext, target, b_t, c_t, tok, taps, heads):
    pairs, rows, chans = target.shape
    out = jax.ShapeDtypeStruct((pairs, DSTATE, chans), F32)
    return pl.pallas_call(
        functools.partial(ends_kernel, heads, rows // SPAN),
        grid=(pairs,),
        out_shape=(out, out),
        in_specs=[per_pair(a.shape[1:]) for a in (x_ext, target, b_t, c_t, tok)] + [whole(taps.shape)],
        out_specs=(per_pair(out.shape[1:]),) * 2,
        scratch_shapes=[pltpu.VMEM((SPAN + HALO, chans), F32)],
        name="ends",
    )(x_ext, target, b_t, c_t, tok, taps)


def main(x_ext, target, b_rows, c_rows, b_t, c_t, tok, table, taps, rate, start, later, heads):
    pairs, rows, chans = target.shape
    count = rows // SPAN
    outs = (
        jax.ShapeDtypeStruct((pairs, rows + HALO, chans), F32),
        jax.ShapeDtypeStruct((pairs, rows, LANES), F32),
        jax.ShapeDtypeStruct((pairs, 8, chans), F32),
    )
    return pl.pallas_call(
        functools.partial(main_kernel, heads, count),
        grid=(pairs,),
        out_shape=outs,
        in_specs=[per_pair(a.shape[1:]) for a in (x_ext, target, b_rows, c_rows, b_t, c_t, tok, table)]
        + [whole(taps.shape), whole(rate.shape)]
        + [per_pair(start.shape[1:])] * 2,
        out_specs=tuple(per_pair(o.shape[1:]) for o in outs),
        scratch_shapes=[
            pltpu.VMEM((SPAN + HALO, chans), F32),
            pltpu.VMEM((count + 1, DSTATE, chans), F32),
            pltpu.VMEM((DSTATE, chans), F32),
            pltpu.VMEM((rows, chans), F32),
            pltpu.VMEM((SPAN, chans), F32),
            pltpu.VMEM((SPAN, chans), F32),
            pltpu.VMEM((TAPS, SPAN + 2 * HALO, chans), F32),
        ],
        name="main",
    )(x_ext, target, b_rows, c_rows, b_t, c_t, tok, table, taps, rate, start, later)


def send(source, goal, sent, got, where):
    return pltpu.make_async_remote_copy(
        src_ref=source,
        dst_ref=goal,
        send_sem=sent,
        recv_sem=got,
        device_id=where,
        device_id_type=pl.DeviceIdType.MESH,
    )


def greet(barrier, where):
    pl.semaphore_signal(barrier, inc=1, device_id=where, device_id_type=pl.DeviceIdType.MESH)


def chain_kernel(axis, through_ref, alone_ref, seed_ref, start_ref, later_ref, out_scr, in_scr, sent, got):
    count = lax.axis_size(axis)
    mine = lax.axis_index(axis)
    pairs, states, chans = alone_ref.shape
    has_less = mine > 0
    has_more = mine < count - 1
    less = lax.rem(mine + count - 1, count)
    more = lax.rem(mine + 1, count)
    barrier = pltpu.get_barrier_semaphore()

    @pl.when(has_less)
    def _():
        greet(barrier, {axis: less})

    @pl.when(has_more)
    def _():
        greet(barrier, {axis: more})

    pl.semaphore_wait(barrier, has_less.astype(jnp.int32) + has_more.astype(jnp.int32))
    ways = ((alone_ref, has_less, has_more, more), (seed_ref, has_more, has_less, less))
    for way, (_, arrives, _, _) in enumerate(ways):

        @pl.when(jnp.logical_not(arrives))
        def _():
            in_scr[way] = jnp.zeros((pairs, states, chans), F32)

    size = states // CUTS
    copies = []
    for b in range(pairs):
        for cut in range(CUTS):
            rows = pl.ds(cut * size, size)
            piece = b * CUTS + cut
            for way, (own, arrives, leaves, goal) in enumerate(ways):
                copy = send(
                    out_scr.at[way, b, rows], in_scr.at[way, b, rows], sent.at[way, piece], got.at[way, piece], {axis: goal}
                )

                @pl.when(arrives)
                def _():
                    copy.wait_recv()

                @pl.when(leaves)
                def _():
                    out_scr[way, b, rows, :] = through_ref[b] * in_scr[way, b, rows, :] + own[b, rows, :]
                    copy.start()

                copies.append((copy, leaves))
    start_ref[...] = in_scr[0]
    later_ref[...] = in_scr[1]
    for copy, leaves in copies:

        @pl.when(leaves)
        def _():
            copy.wait_send()


def chain(through, alone, seed, axis):
    shape = jax.ShapeDtypeStruct(alone.shape, F32)
    vmem = pl.BlockSpec(memory_space=pltpu.VMEM)
    return pl.pallas_call(
        functools.partial(chain_kernel, axis),
        out_shape=(shape, shape),
        in_specs=[vmem] * 3,
        out_specs=(vmem, vmem),
        scratch_shapes=[
            pltpu.VMEM((2,) + alone.shape, F32),
            pltpu.VMEM((2,) + alone.shape, F32),
            pltpu.SemaphoreType.DMA((2, 2 * CUTS)),
            pltpu.SemaphoreType.DMA((2, 2 * CUTS)),
        ],
        compiler_params=pltpu.CompilerParams(collective_id=0, has_side_effects=True),
        name="chain",
    )(through, alone, seed)


def finish_kernel(
    axes, size, grad_ref, score_ref, raw_ref, sign_ref, loss_ref, out_ref, slope_ref,
    part_scr, slot_scr, halo_scr, out_scr, raw_scr, psent, pgot, hsent, hgot, osent, ogot, rsent, rgot,
):
    outer, inner, _ = axes
    pairs, chans = grad_ref.shape[0], grad_ref.shape[2]
    heads = raw_ref.shape[1]
    rows = out_ref.shape[1]
    parts, planes = lax.axis_size(inner), lax.axis_size(outer)
    mine, plane = lax.axis_index(inner), lax.axis_index(outer)
    row = lax.broadcasted_iota(jnp.int32, (8, LANES), 0)
    own = [jnp.sum(jnp.sum(score_ref[b], axis=0, keepdims=True), axis=1, keepdims=True) for b in range(pairs)]
    part_scr[0] = jnp.where(row == 0, own[0], own[1])
    barrier = pltpu.get_barrier_semaphore()
    peers = 0
    for axis in axes:
        for away in range(1, lax.axis_size(axis)):
            greet(barrier, {axis: lax.rem(lax.axis_index(axis) + away, lax.axis_size(axis))})
            peers += 1
    pl.semaphore_wait(barrier, peers)
    has_less = plane > 0
    has_more = plane < planes - 1
    edge = send(
        grad_ref.at[:, pl.ds(0, HALO)], halo_scr, hsent, hgot, {outer: lax.rem(plane + planes - 1, planes)}
    )

    @pl.when(has_less)
    def _():
        edge.start()

    waits = []
    first = 0
    for turn, axis in enumerate(axes[::-1]):
        count = lax.axis_size(axis)
        me = lax.axis_index(axis)
        copies = []
        for away in range(1, count):
            goal = lax.rem(me + away, count)
            spot = first + away - 1
            copy = send(part_scr.at[turn], slot_scr.at[first + me], psent.at[spot], pgot.at[spot], {axis: goal})
            copy.start()
            copies.append(copy)
        slot_scr[first + me] = part_scr[turn]
        for copy in copies:
            copy.wait_recv()
        waits += copies
        subtotal = slot_scr[first]
        for i in range(1, count):
            subtotal = subtotal + slot_scr[first + i]
        part_scr[turn + 1] = subtotal
        first += count
    signed = subtotal * sign_ref[...] / math.sqrt(size)
    margin = signed[0:1, :] + signed[1:2, :]
    loss_ref[...] = jnp.broadcast_to(jax.nn.softplus(-margin), loss_ref.shape)
    factors = -jax.nn.sigmoid(-margin) * sign_ref[...]
    scale = [factors[b : b + 1, 0:1] for b in range(pairs)]

    @pl.when(has_more)
    def _():
        edge.wait_recv()

    @pl.when(jnp.logical_not(has_more))
    def _():
        halo_scr[...] = jnp.zeros_like(halo_scr)

    columns = pl.ds(pl.multiple_of(mine * chans, LANES), chans)
    lines = pl.ds(pl.multiple_of(mine * heads, 8), heads)
    for away in range(parts):
        goal = lax.rem(mine + away, parts) if parts > 1 else 0
        begin = pl.multiple_of(goal * rows, SPAN)
        last = jnp.where(goal == parts - 1, 1.0, 0.0).astype(F32)
        for b in range(pairs):
            body_rows = grad_ref[b, pl.ds(HALO + begin, rows - HALO), :]
            edge_rows = grad_ref[b, pl.ds(begin + rows, HALO), :] + last * halo_scr[b]
            above = (scale[b] * body_rows).astype(BF16)
            below = (scale[b] * edge_rows).astype(BF16)
            lean = scale[b] * raw_ref[b, :, pl.ds(begin, rows)]
            if away == 0:
                out_ref[b, pl.ds(0, rows - HALO), columns] = above
                out_ref[b, pl.ds(rows - HALO, HALO), columns] = below
                slope_ref[b, lines, :] = lean
                continue
            out_scr[away, b, pl.ds(0, rows - HALO), :] = above
            out_scr[away, b, pl.ds(rows - HALO, HALO), :] = below
            raw_scr[away, b] = lean
        if away > 0:
            wide = send(
                out_scr.at[away], out_ref.at[:, :, columns], osent.at[away], ogot.at[away], {inner: goal}
            )
            thin = send(raw_scr.at[away], slope_ref.at[:, lines], rsent.at[away], rgot.at[away], {inner: goal})
            thin.start()
            wide.start()
            waits += [thin, wide]
    for copy in waits[-2 * (parts - 1) :] if parts > 1 else []:
        copy.wait_recv()
    for copy in waits:
        copy.wait_send()

    @pl.when(has_less)
    def _():
        edge.wait_send()


def finish(grad, score, raw, sign, axes, size, rows):
    pairs, chans, heads = grad.shape[0], grad.shape[2], raw.shape[1]
    parts = lax.axis_size(axes[1])
    slots = sum(lax.axis_size(axis) for axis in axes)
    vmem = pl.BlockSpec(memory_space=pltpu.VMEM)
    dma = pltpu.SemaphoreType.DMA
    return pl.pallas_call(
        functools.partial(finish_kernel, axes, size),
        out_shape=(
            jax.ShapeDtypeStruct((8, LANES), F32),
            jax.ShapeDtypeStruct((pairs, rows, parts * chans), BF16),
            jax.ShapeDtypeStruct((pairs, parts * heads, rows), F32),
        ),
        in_specs=[vmem] * 4,
        out_specs=(vmem,) * 3,
        scratch_shapes=[
            pltpu.VMEM((len(axes) + 1, 8, LANES), F32),
            pltpu.VMEM((slots, 8, LANES), F32),
            pltpu.VMEM((pairs, HALO, chans), F32),
            pltpu.VMEM((parts, pairs, rows, chans), BF16),
            pltpu.VMEM((parts, pairs, heads, rows), F32),
            dma((slots,)),
            dma((slots,)),
            dma,
            dma,
            dma((parts,)),
            dma((parts,)),
            dma((parts,)),
            dma((parts,)),
        ],
        compiler_params=pltpu.CompilerParams(collective_id=1, has_side_effects=True),
        name="finish",
    )(grad, score, raw, sign)


def body(outer, inner, x_in, target, b_in, c_in, dt_raw, resets, decay_rate, conv_w, label):
    rows = x_in.shape[1]
    all_heads = dt_raw.shape[1]
    width = x_in.shape[2] // all_heads
    parts = lax.axis_size(inner)
    heads = all_heads // parts
    chans = heads * width
    states = b_in.shape[2] // parts
    tokens = rows * parts
    count = tokens // SPAN
    mine = lax.axis_index(inner)

    def exchange(array):
        if parts == 1:
            return array
        return lax.all_to_all(array, inner, 0, 0, tiled=True)

    def cut(array):
        return array.reshape(2, rows, parts, -1)

    packed = jnp.concatenate([cut(x_in), cut(target), cut(b_in), cut(c_in)], axis=3)
    packed = exchange(packed.transpose(2, 0, 1, 3))
    packed = packed.transpose(1, 0, 2, 3).reshape(2, tokens, -1)
    x_all = packed[:, :, :chans]
    t_all = packed[:, :, chans : 2 * chans]
    b_all = packed[:, :, 2 * chans : 2 * chans + states]
    c_all = packed[:, :, 2 * chans + states :]
    marks = resets.astype(F32)
    small = jnp.concatenate(
        [dt_raw.reshape(2, parts, heads, rows), jnp.broadcast_to(marks[:, None, None, :], (2, parts, 1, rows))], axis=2
    )
    small = exchange(small.transpose(1, 0, 2, 3))
    small = small.transpose(1, 2, 0, 3).reshape(2, heads + 1, tokens)
    raw = small[:, :heads]
    marks = small[:, heads]
    planes = lax.axis_size(outer)
    ahead = [(i, i + 1) for i in range(planes - 1)]
    edge_rows = lax.ppermute(x_all[:, tokens - HALO :], outer, ahead)
    edge_marks = lax.ppermute(marks[:, tokens - 2 :], outer, ahead)
    x_ext = jnp.concatenate([edge_rows, x_all], axis=1)
    keep = 1.0 - jnp.concatenate([edge_marks, marks], axis=1)
    keep_one = keep[:, 2:]
    keep_two = keep_one * keep[:, 1:-1]
    keep_three = keep_two * keep[:, :-2]
    rate = lax.dynamic_slice(decay_rate, (mine * heads,), (heads,))
    taps = lax.dynamic_slice(conv_w, (0, mine * chans), (TAPS, chans))
    steps = jax.nn.softplus(raw)
    logs = -steps * rate[None, :, None]
    upto = jnp.tril(jnp.ones((SPAN, SPAN), F32))
    both = jnp.concatenate([logs, marks[:, None]], axis=1).reshape(2, heads + 1, count, SPAN)
    sums = jnp.einsum("bhkj,ij->bhki", both, upto, precision=HIGH)
    running = sums[:, :heads]
    seen = jnp.round(sums[:, heads:])
    entry = jnp.exp(running) * (seen == 0.0).astype(F32)
    reach = jnp.exp(running[..., -1:] - running) * (seen[..., -1:] == seen).astype(F32)
    through = jnp.prod(entry[..., -1], axis=2)

    def flat(array):
        return array.reshape(2, -1, tokens)

    used = 5 * heads + 4
    table = jnp.concatenate(
        [
            steps,
            flat(entry),
            flat(reach),
            flat(reach) * steps,
            flat(running),
            keep_one[:, None],
            keep_two[:, None],
            keep_three[:, None],
            flat(seen),
            jnp.zeros((2, LANES - used, tokens), F32),
        ],
        axis=1,
    )
    tok = table.transpose(0, 2, 1)
    b_t = b_all.transpose(0, 2, 1)
    c_t = c_all.transpose(0, 2, 1)
    alone, seed = ends(x_ext, t_all, b_t, c_t, tok, taps, heads)
    wide = jnp.repeat(through, width, axis=1)[:, None, :]
    start, later = chain(wide, alone, seed, outer)
    rate_row = jnp.pad(rate, (0, LANES - heads))[None]
    grad, ddt, score = main(x_ext, t_all, b_all, c_all, b_t, c_t, tok, table, taps, rate_row, start, later, heads)
    sign = jnp.where(jnp.arange(2) == label[0], 1.0, -1.0).astype(F32)
    sign = jnp.broadcast_to(jnp.pad(sign, (0, 6))[:, None], (8, LANES))
    size = tokens * planes * x_in.shape[2] * lax.axis_size("head")
    lean = jax.nn.sigmoid(raw) * ddt[:, :, :heads].transpose(0, 2, 1)
    loss, grad, grad_raw = finish(grad, score, lean, sign, (outer, inner, "head"), size, rows)
    return (loss[0, 0], grad, grad_raw)


def solution(mesh):
    def program(*arrays):
        ways, across = mesh.shape["seq"], mesh.shape["head"]
        groups = arrays[2].shape[2] // DSTATE // across
        parts = math.gcd(groups, ways)
        devices = mesh.devices.reshape(ways // parts, parts, across)
        finer = Mesh(devices, ("outer", "inner", "head"))
        seq = ("outer", "inner")
        in_specs = (
            P(None, seq, "head"),
            P(None, seq, "head"),
            P(None, seq, "head"),
            P(None, seq, "head"),
            P(None, "head", seq),
            P(None, seq),
            P("head"),
            P(None, "head"),
            P(),
        )
        out_specs = (P(), P(None, seq, "head"), P(None, "head", seq))
        inner = functools.partial(body, "outer", "inner")
        mapped = jax.shard_map(inner, mesh=finer, in_specs=in_specs, out_specs=out_specs, check_vma=False)
        return mapped(*arrays)

    return program
```

```python
import functools
import math

import jax
import jax.numpy as jnp
from jax import lax
from jax.experimental import pallas as pl
from jax.experimental.pallas import tpu as pltpu
from jax.sharding import Mesh
from jax.sharding import PartitionSpec as P

DSTATE = 128
SPAN = 128
LANES = 128
TAPS = 4
CUTS = 4
HALO = 16
FAR = -1e30
HIGH = lax.Precision.HIGHEST
F32 = jnp.float32
BF16 = jnp.bfloat16


def split(value):
    high = value.astype(BF16)
    low = (value - high.astype(F32)).astype(BF16)
    return high, low


def mm(left, right):
    return lax.dot_general(left, right, (((1,), (0,)), ((), ())), preferred_element_type=F32)


def mm_exact_left(left, right):
    high, low = split(right)
    return mm(left, high) + mm(left, low)


def mm_exact_right(left, right):
    high, low = split(left)
    return mm(high, right) + mm(low, right)


def spread_matrix(offset, chans, width):
    row = lax.broadcasted_iota(jnp.int32, (LANES, chans), 0)
    head = lax.broadcasted_iota(jnp.int32, (LANES, chans), 1) // width
    return jnp.where(row == head + offset, 1.0, 0.0).astype(BF16)


def gather_matrix(chans, width):
    head = lax.broadcasted_iota(jnp.int32, (chans, LANES), 0) // width
    col = lax.broadcasted_iota(jnp.int32, (chans, LANES), 1)
    return jnp.where(col == head, 1.0, 0.0).astype(BF16)


def conv_of(x_ref, xe_scr, w_ref, tok, lane, first):
    xe_scr[...] = x_ref[pl.ds(first, SPAN + HALO), :].astype(F32)
    pre = w_ref[3:4, :] * xe_scr[pl.ds(HALO, SPAN), :]
    for back in range(1, TAPS):
        scale = tok[:, lane + back - 1 : lane + back] * w_ref[3 - back : 4 - back, :]
        pre = pre + scale * xe_scr[pl.ds(HALO - back, SPAN), :]
    return pre


def ends_kernel(heads, count, x_ref, t_ref, bt_ref, ct_ref, tok_ref, w_ref, alone_ref, seed_ref, xe_scr):
    chans = x_ref.shape[1]
    width = chans // heads
    spread_entry = spread_matrix(heads, chans, width)
    spread_tail = spread_matrix(3 * heads, chans, width)
    alone_ref[...] = jnp.zeros_like(alone_ref)
    seed_ref[...] = jnp.zeros_like(seed_ref)

    def forward(k, carry):
        first = pl.multiple_of(k * SPAN, SPAN)
        tok = tok_ref[pl.ds(first, SPAN), :]
        values = jax.nn.silu(conv_of(x_ref, xe_scr, w_ref, tok, 5 * heads, first))
        weighted = values * mm_exact_right(tok, spread_tail)
        through = mm_exact_right(tok[SPAN - 8 :, :], spread_entry)[7:8, :]
        added = mm_exact_left(bt_ref[:, pl.ds(first, SPAN)], weighted)
        alone_ref[...] = through * alone_ref[...] + added
        return carry

    lax.fori_loop(0, count, forward, 0)

    def backward(step, carry):
        first = pl.multiple_of((count - 1 - step) * SPAN, SPAN)
        tok = tok_ref[pl.ds(first, SPAN), :]
        entry = mm_exact_right(tok, spread_entry)
        weighted = entry * t_ref[pl.ds(first, SPAN), :].astype(F32)
        added = mm_exact_left(ct_ref[:, pl.ds(first, SPAN)], weighted)
        seed_ref[...] = entry[SPAN - 1 : SPAN, :] * seed_ref[...] + added
        return carry

    lax.fori_loop(0, count, backward, 0)


def main_kernel(
    heads, count, x_ref, t_ref, b_ref, c_ref, bt_ref, ct_ref, tok_ref, row_ref, w_ref, rate_ref,
    start_ref, later_ref, grad_ref, ddt_ref, score_ref, xe_scr, s_scr, g_scr, v_scr, y_scr, d_scr, cv_scr,
):
    chans = x_ref.shape[1]
    width = chans // heads
    per = LANES // width
    spread_steps = spread_matrix(0, chans, width)
    spread_entry = spread_matrix(heads, chans, width)
    spread_reach = spread_matrix(2 * heads, chans, width)
    spread_tail = spread_matrix(3 * heads, chans, width)
    gather = gather_matrix(chans, width)
    s_scr[0] = start_ref[...]
    g_scr[...] = later_ref[...]
    score_ref[...] = jnp.zeros_like(score_ref)
    cv_scr[...] = jnp.zeros_like(cv_scr)
    total = count * SPAN
    grad_ref[pl.ds(total, HALO), :] = jnp.zeros((HALO, chans), F32)

    def forward(k, carry):
        first = pl.multiple_of(k * SPAN, SPAN)
        tok = tok_ref[pl.ds(first, SPAN), :]
        pre = conv_of(x_ref, xe_scr, w_ref, tok, 5 * heads, first)
        v_scr[pl.ds(first, SPAN), :] = pre
        weighted = jax.nn.silu(pre) * mm_exact_right(tok, spread_tail)
        through = mm_exact_right(tok[SPAN - 8 :, :], spread_entry)[7:8, :]
        added = mm_exact_left(bt_ref[:, pl.ds(first, SPAN)], weighted)
        s_scr[k + 1] = through * s_scr[k] + added
        return carry

    lax.fori_loop(0, count, forward, 0)

    def backward(step, carry):
        k = count - 1 - step
        first = pl.multiple_of(k * SPAN, SPAN)
        here = pl.ds(first, SPAN)
        tok = tok_ref[here, :]
        pre = v_scr[here, :]
        sig = jax.nn.sigmoid(pre)
        values = pre * sig
        slope = sig * (1.0 + pre * (1.0 - sig))
        target = t_ref[here, :]
        b_rows = b_ref[here, :]
        c_rows = c_ref[here, :]
        bt = bt_ref[:, here]
        ct = ct_ref[:, here]
        steps = mm_exact_right(tok, spread_steps)
        entry = mm_exact_right(tok, spread_entry)
        reach = mm_exact_right(tok, spread_reach)
        y_scr[...] = entry * mm_exact_left(c_rows, s_scr[k])
        d_scr[...] = reach * mm_exact_left(b_rows, g_scr[...])
        u_high, u_low = split(steps * values)
        scores = mm(c_rows, bt)
        scores_t = mm(b_rows, ct)
        seen_col = tok[:, 5 * heads + 3 : 5 * heads + 4]
        seen_row = row_ref[5 * heads + 3 : 5 * heads + 4, here]
        order_row = lax.broadcasted_iota(jnp.int32, (SPAN, SPAN), 0)
        order_col = lax.broadcasted_iota(jnp.int32, (SPAN, SPAN), 1)
        same = seen_col == seen_row
        valid = same & (order_row >= order_col)
        valid_t = same & (order_row <= order_col)
        lane = lax.broadcasted_iota(jnp.int32, (SPAN, LANES), 1) // width
        for unit in range(heads // per):
            cols = slice(unit * LANES, (unit + 1) * LANES)
            t_unit = target[:, cols]
            both = jnp.concatenate([u_high[:, cols], u_low[:, cols]], axis=1)
            y_unit = jnp.zeros((SPAN, LANES), F32)
            d_unit = jnp.zeros((SPAN, LANES), F32)
            for part in range(per):
                h = 4 * heads + unit * per + part
                r_col = tok[:, h : h + 1]
                r_row = row_ref[h : h + 1, here]
                gap = r_col - r_row
                mix = jnp.exp(jnp.where(valid, gap, FAR)) * scores
                mix_t = jnp.exp(jnp.where(valid_t, -gap, FAR)) * scores_t
                m_high, m_low = split(mix)
                n_high, n_low = split(mix_t)
                wide = mm(m_high, both)
                y_part = wide[:, :LANES] + wide[:, LANES:] + mm(m_low, both[:, :LANES])
                d_part = mm(n_high, t_unit) + mm(n_low, t_unit)
                y_unit = jnp.where(lane == part, y_part, y_unit)
                d_unit = jnp.where(lane == part, d_part, d_unit)
            y_scr[:, cols] += y_unit
            d_scr[:, cols] += d_unit
        target_f = target.astype(F32)
        read = y_scr[...] * target_f
        score_ref[...] += jnp.sum(read.reshape(SPAN // 8, 8, chans), axis=0)
        du = d_scr[...]
        by_read = mm_exact_right(read, gather)
        by_step = mm_exact_right(values * du, gather)
        cross = jnp.sum((s_scr[k + 1] * g_scr[...]).reshape(DSTATE // 8, 8, chans), axis=0)
        crossed = jnp.sum(mm_exact_right(cross, gather), axis=0, keepdims=True)
        upper = jnp.where(order_row <= order_col, 1.0, 0.0).astype(BF16)
        d_log = mm_exact_left(upper, by_read - tok * by_step) + crossed
        ddt_ref[here, :] = by_step - rate_ref[...] * d_log
        d_pre = steps * du * slope
        cv_scr[0, pl.ds(HALO, SPAN), :] = w_ref[3:4, :] * d_pre
        for back in range(1, TAPS):
            scale = tok[:, 5 * heads + back - 1 : 5 * heads + back] * w_ref[3 - back : 4 - back, :]
            cv_scr[back, pl.ds(HALO, SPAN), :] = scale * d_pre
        top = cv_scr[0, pl.ds(0, SPAN), :]
        end = cv_scr[0, pl.ds(SPAN, HALO), :]
        for back in range(1, TAPS):
            top = top + cv_scr[back, pl.ds(back, SPAN), :]
            end = end + cv_scr[back, pl.ds(SPAN + back, HALO), :]
        grad_ref[here, :] = top
        tail = pl.ds(pl.multiple_of(first + SPAN, SPAN), HALO)
        grad_ref[tail, :] += end
        weighted = entry * target_f
        g_scr[...] = entry[SPAN - 1 : SPAN, :] * g_scr[...] + mm_exact_left(ct, weighted)
        return carry

    lax.fori_loop(0, count, backward, 0)


def per_pair(shape):
    return pl.BlockSpec((None,) + tuple(shape), lambda b: (b,) + (0,) * len(shape))


def whole(shape):
    return pl.BlockSpec(tuple(shape), lambda b: (0,) * len(shape))


def ends(x_ext, target, b_t, c_t, tok, taps, heads):
    pairs, rows, chans = target.shape
    out = jax.ShapeDtypeStruct((pairs, DSTATE, chans), F32)
    return pl.pallas_call(
        functools.partial(ends_kernel, heads, rows // SPAN),
        grid=(pairs,),
        out_shape=(out, out),
        in_specs=[per_pair(a.shape[1:]) for a in (x_ext, target, b_t, c_t, tok)] + [whole(taps.shape)],
        out_specs=(per_pair(out.shape[1:]),) * 2,
        scratch_shapes=[pltpu.VMEM((SPAN + HALO, chans), F32)],
        name="ends",
    )(x_ext, target, b_t, c_t, tok, taps)


def main(x_ext, target, b_rows, c_rows, b_t, c_t, tok, table, taps, rate, start, later, heads):
    pairs, rows, chans = target.shape
    count = rows // SPAN
    outs = (
        jax.ShapeDtypeStruct((pairs, rows + HALO, chans), F32),
        jax.ShapeDtypeStruct((pairs, rows, LANES), F32),
        jax.ShapeDtypeStruct((pairs, 8, chans), F32),
    )
    return pl.pallas_call(
        functools.partial(main_kernel, heads, count),
        grid=(pairs,),
        out_shape=outs,
        in_specs=[per_pair(a.shape[1:]) for a in (x_ext, target, b_rows, c_rows, b_t, c_t, tok, table)]
        + [whole(taps.shape), whole(rate.shape)]
        + [per_pair(start.shape[1:])] * 2,
        out_specs=tuple(per_pair(o.shape[1:]) for o in outs),
        scratch_shapes=[
            pltpu.VMEM((SPAN + HALO, chans), F32),
            pltpu.VMEM((count + 1, DSTATE, chans), F32),
            pltpu.VMEM((DSTATE, chans), F32),
            pltpu.VMEM((rows, chans), F32),
            pltpu.VMEM((SPAN, chans), F32),
            pltpu.VMEM((SPAN, chans), F32),
            pltpu.VMEM((TAPS, SPAN + 2 * HALO, chans), F32),
        ],
        name="main",
    )(x_ext, target, b_rows, c_rows, b_t, c_t, tok, table, taps, rate, start, later)


def send(source, goal, sent, got, where):
    return pltpu.make_async_remote_copy(
        src_ref=source,
        dst_ref=goal,
        send_sem=sent,
        recv_sem=got,
        device_id=where,
        device_id_type=pl.DeviceIdType.MESH,
    )


def greet(barrier, where):
    pl.semaphore_signal(barrier, inc=1, device_id=where, device_id_type=pl.DeviceIdType.MESH)


def chain_kernel(axis, through_ref, alone_ref, seed_ref, start_ref, later_ref, out_scr, in_scr, sent, got):
    count = lax.axis_size(axis)
    mine = lax.axis_index(axis)
    own_pieces, size, chans = alone_ref.shape
    has_less = mine > 0
    has_more = mine < count - 1
    less = lax.rem(mine + count - 1, count)
    more = lax.rem(mine + 1, count)
    barrier = pltpu.get_barrier_semaphore()

    @pl.when(has_less)
    def _():
        greet(barrier, {axis: less})

    @pl.when(has_more)
    def _():
        greet(barrier, {axis: more})

    pl.semaphore_wait(barrier, has_less.astype(jnp.int32) + has_more.astype(jnp.int32))
    ways = ((alone_ref, has_less, has_more, more), (seed_ref, has_more, has_less, less))
    for way, (_, arrives, _, _) in enumerate(ways):

        @pl.when(jnp.logical_not(arrives))
        def _():
            in_scr[way] = jnp.zeros((own_pieces, size, chans), F32)

    pieces = own_pieces

    def hop(time, carry):
        for way, (own, arrives, leaves, goal) in enumerate(ways):
            piece = time - (mine if way == 0 else count - 1 - mine)

            @pl.when((piece >= 0) & (piece < pieces))
            def _():
                copy = send(
                    out_scr.at[way, piece], in_scr.at[way, piece], sent.at[way, piece], got.at[way, piece], {axis: goal}
                )

                @pl.when(arrives)
                def _():
                    copy.wait_recv()

                @pl.when(leaves)
                def _():
                    through = through_ref[piece // CUTS]
                    out_scr[way, piece] = through * in_scr[way, piece] + own[piece]
                    copy.start()

        return carry

    lax.fori_loop(0, pieces + count - 1, hop, 0)
    start_ref[...] = in_scr[0]
    later_ref[...] = in_scr[1]

    def drain(piece, carry):
        for way, (_, _, leaves, goal) in enumerate(ways):

            @pl.when(leaves)
            def _():
                send(
                    out_scr.at[way, piece], in_scr.at[way, piece], sent.at[way, piece], got.at[way, piece], {axis: goal}
                ).wait_send()

        return carry

    lax.fori_loop(0, pieces, drain, 0)


def chain(through, alone, seed, axis):
    whole_shape = alone.shape
    pieces = whole_shape[0] * CUTS
    alone = alone.reshape(pieces, -1, whole_shape[2])
    seed = seed.reshape(alone.shape)
    shape = jax.ShapeDtypeStruct(alone.shape, F32)
    vmem = pl.BlockSpec(memory_space=pltpu.VMEM)
    start, later = pl.pallas_call(
        functools.partial(chain_kernel, axis),
        out_shape=(shape, shape),
        in_specs=[vmem] * 3,
        out_specs=(vmem, vmem),
        scratch_shapes=[
            pltpu.VMEM((2,) + alone.shape, F32),
            pltpu.VMEM((2,) + alone.shape, F32),
            pltpu.SemaphoreType.DMA((2, pieces)),
            pltpu.SemaphoreType.DMA((2, pieces)),
        ],
        compiler_params=pltpu.CompilerParams(collective_id=0, has_side_effects=True),
        name="chain",
    )(through, alone, seed)
    return start.reshape(whole_shape), later.reshape(whole_shape)


def finish_kernel(
    axes, size, grad_ref, score_ref, raw_ref, sign_ref, loss_ref, out_ref, slope_ref,
    part_scr, slot_scr, halo_scr, out_scr, raw_scr, psent, pgot, hsent, hgot, osent, ogot, rsent, rgot,
):
    outer, inner, _ = axes
    pairs, chans = grad_ref.shape[0], grad_ref.shape[2]
    heads = raw_ref.shape[1]
    rows = out_ref.shape[1]
    parts, planes = lax.axis_size(inner), lax.axis_size(outer)
    mine, plane = lax.axis_index(inner), lax.axis_index(outer)
    row = lax.broadcasted_iota(jnp.int32, (8, LANES), 0)
    own = [jnp.sum(jnp.sum(score_ref[b], axis=0, keepdims=True), axis=1, keepdims=True) for b in range(pairs)]
    part_scr[0] = jnp.where(row == 0, own[0], own[1])
    barrier = pltpu.get_barrier_semaphore()
    peers = 0
    for axis in axes:
        for away in range(1, lax.axis_size(axis)):
            greet(barrier, {axis: lax.rem(lax.axis_index(axis) + away, lax.axis_size(axis))})
            peers += 1
    pl.semaphore_wait(barrier, peers)
    has_less = plane > 0
    has_more = plane < planes - 1
    edge = send(
        grad_ref.at[:, pl.ds(0, HALO)], halo_scr, hsent, hgot, {outer: lax.rem(plane + planes - 1, planes)}
    )

    @pl.when(has_less)
    def _():
        edge.start()

    waits = []
    first = 0
    for turn, axis in enumerate(axes[::-1]):
        count = lax.axis_size(axis)
        me = lax.axis_index(axis)
        copies = []
        for away in range(1, count):
            goal = lax.rem(me + away, count)
            spot = first + away - 1
            copy = send(part_scr.at[turn], slot_scr.at[first + me], psent.at[spot], pgot.at[spot], {axis: goal})
            copy.start()
            copies.append(copy)
        slot_scr[first + me] = part_scr[turn]
        for copy in copies:
            copy.wait_recv()
        waits += copies
        subtotal = slot_scr[first]
        for i in range(1, count):
            subtotal = subtotal + slot_scr[first + i]
        part_scr[turn + 1] = subtotal
        first += count
    signed = subtotal * sign_ref[...] / math.sqrt(size)
    margin = signed[0:1, :] + signed[1:2, :]
    loss_ref[...] = jnp.broadcast_to(jax.nn.softplus(-margin), loss_ref.shape)
    factors = -jax.nn.sigmoid(-margin) * sign_ref[...]
    scale = [factors[b : b + 1, 0:1] for b in range(pairs)]

    @pl.when(has_more)
    def _():
        edge.wait_recv()

    @pl.when(jnp.logical_not(has_more))
    def _():
        halo_scr[...] = jnp.zeros_like(halo_scr)

    columns = pl.ds(pl.multiple_of(mine * chans, LANES), chans)
    lines = pl.ds(pl.multiple_of(mine * heads, 8), heads)
    for away in range(parts):
        goal = lax.rem(mine + away, parts) if parts > 1 else 0
        begin = pl.multiple_of(goal * rows, SPAN)
        last = jnp.where(goal == parts - 1, 1.0, 0.0).astype(F32)
        for b in range(pairs):
            body_rows = grad_ref[b, pl.ds(HALO + begin, rows - HALO), :]
            edge_rows = grad_ref[b, pl.ds(begin + rows, HALO), :] + last * halo_scr[b]
            above = (scale[b] * body_rows).astype(BF16)
            below = (scale[b] * edge_rows).astype(BF16)
            lean = scale[b] * raw_ref[b, :, pl.ds(begin, rows)]
            if away == 0:
                out_ref[b, pl.ds(0, rows - HALO), columns] = above
                out_ref[b, pl.ds(rows - HALO, HALO), columns] = below
                slope_ref[b, lines, :] = lean
                continue
            out_scr[away, b, pl.ds(0, rows - HALO), :] = above
            out_scr[away, b, pl.ds(rows - HALO, HALO), :] = below
            raw_scr[away, b] = lean
        if away > 0:
            wide = send(
                out_scr.at[away], out_ref.at[:, :, columns], osent.at[away], ogot.at[away], {inner: goal}
            )
            thin = send(raw_scr.at[away], slope_ref.at[:, lines], rsent.at[away], rgot.at[away], {inner: goal})
            thin.start()
            wide.start()
            waits += [thin, wide]
    for copy in waits[-2 * (parts - 1) :] if parts > 1 else []:
        copy.wait_recv()
    for copy in waits:
        copy.wait_send()

    @pl.when(has_less)
    def _():
        edge.wait_send()


def finish(grad, score, raw, sign, axes, size, rows):
    pairs, chans, heads = grad.shape[0], grad.shape[2], raw.shape[1]
    parts = lax.axis_size(axes[1])
    slots = sum(lax.axis_size(axis) for axis in axes)
    vmem = pl.BlockSpec(memory_space=pltpu.VMEM)
    dma = pltpu.SemaphoreType.DMA
    return pl.pallas_call(
        functools.partial(finish_kernel, axes, size),
        out_shape=(
            jax.ShapeDtypeStruct((8, LANES), F32),
            jax.ShapeDtypeStruct((pairs, rows, parts * chans), BF16),
            jax.ShapeDtypeStruct((pairs, parts * heads, rows), F32),
        ),
        in_specs=[vmem] * 4,
        out_specs=(vmem,) * 3,
        scratch_shapes=[
            pltpu.VMEM((len(axes) + 1, 8, LANES), F32),
            pltpu.VMEM((slots, 8, LANES), F32),
            pltpu.VMEM((pairs, HALO, chans), F32),
            pltpu.VMEM((parts, pairs, rows, chans), BF16),
            pltpu.VMEM((parts, pairs, heads, rows), F32),
            dma((slots,)),
            dma((slots,)),
            dma,
            dma,
            dma((parts,)),
            dma((parts,)),
            dma((parts,)),
            dma((parts,)),
        ],
        compiler_params=pltpu.CompilerParams(collective_id=1, has_side_effects=True),
        name="finish",
    )(grad, score, raw, sign)


def body(outer, inner, x_in, target, b_in, c_in, dt_raw, resets, decay_rate, conv_w, label):
    rows = x_in.shape[1]
    all_heads = dt_raw.shape[1]
    width = x_in.shape[2] // all_heads
    parts = lax.axis_size(inner)
    heads = all_heads // parts
    chans = heads * width
    states = b_in.shape[2] // parts
    tokens = rows * parts
    count = tokens // SPAN
    mine = lax.axis_index(inner)

    def exchange(array):
        if parts == 1:
            return array
        return lax.all_to_all(array, inner, 0, 0, tiled=True)

    def cut(array):
        return array.reshape(2, rows, parts, -1)

    packed = jnp.concatenate([cut(x_in), cut(target), cut(b_in), cut(c_in)], axis=3)
    packed = exchange(packed.transpose(2, 0, 1, 3))
    packed = packed.transpose(1, 0, 2, 3).reshape(2, tokens, -1)
    x_all = packed[:, :, :chans]
    t_all = packed[:, :, chans : 2 * chans]
    b_all = packed[:, :, 2 * chans : 2 * chans + states]
    c_all = packed[:, :, 2 * chans + states :]
    marks = resets.astype(F32)
    small = jnp.concatenate(
        [dt_raw.reshape(2, parts, heads, rows), jnp.broadcast_to(marks[:, None, None, :], (2, parts, 1, rows))], axis=2
    )
    small = exchange(small.transpose(1, 0, 2, 3))
    small = small.transpose(1, 2, 0, 3).reshape(2, heads + 1, tokens)
    raw = small[:, :heads]
    marks = small[:, heads]
    planes = lax.axis_size(outer)
    ahead = [(i, i + 1) for i in range(planes - 1)]
    edge_rows = lax.ppermute(x_all[:, tokens - HALO :], outer, ahead)
    edge_marks = lax.ppermute(marks[:, tokens - 2 :], outer, ahead)
    x_ext = jnp.concatenate([edge_rows, x_all], axis=1)
    keep = 1.0 - jnp.concatenate([edge_marks, marks], axis=1)
    keep_one = keep[:, 2:]
    keep_two = keep_one * keep[:, 1:-1]
    keep_three = keep_two * keep[:, :-2]
    rate = lax.dynamic_slice(decay_rate, (mine * heads,), (heads,))
    taps = lax.dynamic_slice(conv_w, (0, mine * chans), (TAPS, chans))
    steps = jax.nn.softplus(raw)
    logs = -steps * rate[None, :, None]
    upto = jnp.tril(jnp.ones((SPAN, SPAN), F32))
    both = jnp.concatenate([logs, marks[:, None]], axis=1).reshape(2, heads + 1, count, SPAN)
    sums = jnp.einsum("bhkj,ij->bhki", both, upto, precision=HIGH)
    running = sums[:, :heads]
    seen = jnp.round(sums[:, heads:])
    entry = jnp.exp(running) * (seen == 0.0).astype(F32)
    reach = jnp.exp(running[..., -1:] - running) * (seen[..., -1:] == seen).astype(F32)
    through = jnp.prod(entry[..., -1], axis=2)

    def flat(array):
        return array.reshape(2, -1, tokens)

    used = 5 * heads + 4
    table = jnp.concatenate(
        [
            steps,
            flat(entry),
            flat(reach),
            flat(reach) * steps,
            flat(running),
            keep_one[:, None],
            keep_two[:, None],
            keep_three[:, None],
            flat(seen),
            jnp.zeros((2, LANES - used, tokens), F32),
        ],
        axis=1,
    )
    tok = table.transpose(0, 2, 1)
    b_t = b_all.transpose(0, 2, 1)
    c_t = c_all.transpose(0, 2, 1)
    alone, seed = ends(x_ext, t_all, b_t, c_t, tok, taps, heads)
    wide = jnp.repeat(through, width, axis=1)[:, None, :]
    start, later = chain(wide, alone, seed, outer)
    rate_row = jnp.pad(rate, (0, LANES - heads))[None]
    grad, ddt, score = main(x_ext, t_all, b_all, c_all, b_t, c_t, tok, table, taps, rate_row, start, later, heads)
    sign = jnp.where(jnp.arange(2) == label[0], 1.0, -1.0).astype(F32)
    sign = jnp.broadcast_to(jnp.pad(sign, (0, 6))[:, None], (8, LANES))
    size = tokens * planes * x_in.shape[2] * lax.axis_size("head")
    lean = jax.nn.sigmoid(raw) * ddt[:, :, :heads].transpose(0, 2, 1)
    loss, grad, grad_raw = finish(grad, score, lean, sign, (outer, inner, "head"), size, rows)
    return (loss[0, 0], grad, grad_raw)


def solution(mesh):
    def program(*arrays):
        ways, across = mesh.shape["seq"], mesh.shape["head"]
        groups = arrays[2].shape[2] // DSTATE // across
        parts = math.gcd(groups, ways)
        devices = mesh.devices.reshape(ways // parts, parts, across)
        finer = Mesh(devices, ("outer", "inner", "head"))
        seq = ("outer", "inner")
        in_specs = (
            P(None, seq, "head"),
            P(None, seq, "head"),
            P(None, seq, "head"),
            P(None, seq, "head"),
            P(None, "head", seq),
            P(None, seq),
            P("head"),
            P(None, "head"),
            P(),
        )
        out_specs = (P(), P(None, seq, "head"), P(None, "head", seq))
        inner = functools.partial(body, "outer", "inner")
        mapped = jax.shard_map(inner, mesh=finer, in_specs=in_specs, out_specs=out_specs, check_vma=False)
        return mapped(*arrays)

    return program
```
